32 devices in a mesh: beam: 8 (over z, y), elem: 4 (over x, core).
Axes of the slice: x: 2, y: 2, z: 4, core: 2. Of those that a mesh axis runs over, the one named last changes fastest.
Arguments:
- signals: bfloat16 [2, 16384, 256], P(None, 'elem', 'beam'), may hold values from -6 to 6
- weights: bfloat16 [2, 16384, 16384], P(None, 'beam', 'elem'), may hold values from -0.0625 to 0.0625
- element_flags: int32 [16384], P('elem'), may hold values from 0 to 1, as said below
Outputs:
- beam_out: bfloat16 [2, 16384, 256], P(None, ('beam', 'elem'))
- beam_power: float32 [16384], P(('beam', 'elem'))
The draws below stay inside these ranges and needn't reach their ends.
Inputs may be any that keep to these rules, and one draw needn't show every extreme that they name: `element_flags`: element 16384 - 1 is always live.
All inputs are finite; a program needn't handle non-finite values.
Results may differ from the reference program's by a relative error of at most 0.001.
Values may be sent and summed in bfloat16 or wider, within the bound.
A program may use at most 128 MiB of HBM per device.

```python
import jax
import jax.numpy as jnp
from jax import lax

B = 16384
E = 16384
T_SIZE = 256


def draw_element_flags(key, part):
    positions = jnp.arange(E, dtype=jnp.int32)
    levels = jax.random.randint(key, (E,), 0, 1000, dtype=jnp.int32)
    threshold = 300 + 650 * positions // E
    alive = (levels < threshold) | (positions == E - 1)
    return alive.astype(jnp.int32)


def strengthened(array, rng, source, target, shards_of, factor):
    def block_of(axis_at):
        return (jnp.arange(array.shape[axis_at]) // (array.shape[axis_at] // shards_of)).reshape((-1,) + (1,) * (array.ndim - 1 - axis_at))

    one_side = jax.random.permutation(rng, shards_of)[block_of(target)]
    far = (block_of(target) + shards_of // 2) % shards_of
    return jnp.where((block_of(source) == one_side) | (block_of(source) == far), factor * array, array)


def steps_of(own_key, shape, split, least, top_value):
    gain, own = 1.0, jax.random.fold_in(own_key, 6)
    for position, blocks in split:
        heights = jnp.exp(jax.random.uniform(jax.random.fold_in(own, position), (blocks,), jnp.float32, least / len(split), top_value / len(split)))
        gain = gain * jnp.repeat(heights, shape[position] // blocks).reshape([-1 if axis == position else 1 for axis in range(len(shape))])
    return gain


def bell_draw(rng, extent, scale, most, split=(), kind=jnp.bfloat16):
    array = jax.random.normal(rng, extent, jnp.float32) * scale
    if len(split) > 0:
        array = steps_of(rng, extent, split, -0.22, 0.18) * array
    return jnp.clip(array, min=-most, max=most).astype(kind)


def gaussian_with(rng, extent, width, reach, shards, heavy, kind=jnp.bfloat16):
    array = width * jax.random.normal(rng, extent, jnp.float32)
    if shards:
        array = array * steps_of(rng, extent, shards, -0.22, 0.18)
    return jnp.clip(strengthened(array, jax.random.fold_in(rng, 3), *heavy), -reach, reach).astype(kind)


def setup_inputs(seed: int = 0) -> dict:
    keys = jax.random.split(jax.random.key(seed), 4)
    return {
        "signals": bell_draw(keys[0], (2, E, T_SIZE), 1.0, 6.0, ((1, 4), (2, 8))),
        "weights": gaussian_with(keys[1], (2, B, E), E ** -0.5, 0.0625, ((1, 8), (2, 4)), (2, 1, 8, 2.0)),
        "element_flags": draw_element_flags(jax.random.fold_in(keys[3], 71), 0),
    }


def reference(signals, weights, element_flags):
    masked = signals * element_flags.astype(jnp.bfloat16)[None, :, None]
    live_total = jnp.sum(element_flags.astype(jnp.float32))
    beam_gain = jnp.sqrt(jnp.float32(E) / live_total)
    real_part = jnp.dot(weights[0], masked[0], preferred_element_type=jnp.float32) - jnp.dot(weights[1], masked[1], preferred_element_type=jnp.float32)
    imag_part = jnp.dot(weights[0], masked[1], preferred_element_type=jnp.float32) + jnp.dot(weights[1], masked[0], preferred_element_type=jnp.float32)
    scaled = jnp.stack([real_part, imag_part]) * beam_gain
    beam_out = scaled.astype(jnp.bfloat16)
    beam_power = lax.optimization_barrier(jnp.mean(scaled[0] * scaled[0] + scaled[1] * scaled[1], axis=1))
    return (beam_out, beam_power)
```

```python
import functools

import jax
import jax.numpy as jnp
from jax import lax
from jax.experimental import pallas as pl
from jax.experimental.pallas import tpu as pltpu
from jax.sharding import PartitionSpec as P

PIECES = 8
LANES = 128
MESH = pl.DeviceIdType.MESH


def ring_order(mesh):
    nb = mesh.shape["beam"]
    try:
        coords = [tuple(d.coords) for d in mesh.devices[:, 0]]
    except AttributeError:
        return list(range(nb))
    axes = [a for a in range(len(coords[0])) if len({c[a] for c in coords}) > 1]
    if len(axes) != 2:
        return list(range(nb))
    values = [sorted({c[a] for c in coords}) for a in axes]
    if len(values[0]) % 2:
        axes, values = axes[::-1], values[::-1]
    rows, cols = len(values[0]), len(values[1])
    if rows % 2 or rows * cols != nb:
        return list(range(nb))
    at = {(values[0].index(c[axes[0]]), values[1].index(c[axes[1]])): i for i, c in enumerate(coords)}
    path = [(0, 0)]
    for r in range(rows):
        inner = range(1, cols) if r % 2 == 0 else range(cols - 1, 0, -1)
        path += [(r, c) for c in inner]
    path += [(r, 0) for r in range(rows - 1, 0, -1)]
    return [at[p] for p in path]


def lookup(table, index):
    value = jnp.int32(table[0])
    for i in range(1, len(table)):
        value = jnp.where(index == i, jnp.int32(table[i]), value)
    return value


def kernel(order, ne, s_ref, flag_ref, w_ref, out_ref, pow_ref,
           blocks, flags, mask, weights, rhs, xpart, opart, first, ofirst, second, counts, select, values, square,
           ring_send, ring_recv, w_sem, s_sem, f_sem, first_send, first_recv, ofirst_send, ofirst_recv,
           second_send, second_recv, cnt_send, cnt_recv):
    nb = len(order)
    half = nb // 2
    _, tb, depth = s_ref.shape
    q = PIECES
    step = max(1, q // 4)
    kq = depth // q
    mo = opart.shape[2]
    ways = ne // 2
    snaps = nb * tb
    blk = 2 * tb

    me_b = lax.axis_index("beam")
    me_e = lax.axis_index("elem")
    inverse = [order.index(i) for i in range(nb)]
    pos = lookup(inverse, me_b)
    ahead = lookup([order[(inverse[i] + 1) % nb] for i in range(nb)], me_b)
    behind = lookup([order[(inverse[i] - 1) % nb] for i in range(nb)], me_b)
    core = lax.rem(me_e, 2)
    mine = me_e // 2
    partner = me_e + 1 - 2 * core

    def slot_of(way, d):
        return d if (way == 0 or d in (0, half)) else half + d

    def unit_columns(u):
        if u == 0:
            return [(0, 0), (0, 1)]
        if u == 1:
            return [(1, 1), (1, 1)]
        if u == half:
            return [(0, half), (0, half)]
        return [(1, u), (0, u)]

    def folded(u):
        return u in (1, half)

    def place(u):
        return 1 if u == half else u

    def rows_of(u):
        return pl.ds(mo // 2 if u == half else 0, mo // 2 if folded(u) else mo)

    def pair_columns(p):
        return [(0, 0), (0, 1)] if p == 0 else [(1, p), (0, p + 1)]

    def units_of(d):
        return [0, 1] if d == 1 else [d]

    low, high = q // 2, q // 2
    arrivals = [[(d, j) for d in range(1, half) for j in range(q)] + [(half, j) for j in last]
                for last in (range(q - 1, high - 1, -1), range(low))]
    number = [{item: k for k, item in enumerate(a)} for a in arrivals]

    def ring_copy(way, d, j):
        k = number[way][(d, j)]
        return pltpu.make_async_remote_copy(
            src_ref=(s_ref if d == 1 else blocks.at[slot_of(way, d - 1)]).at[:, :, pl.ds(j * kq, kq)],
            dst_ref=blocks.at[slot_of(way, d), :, :, pl.ds(j * kq, kq)],
            send_sem=ring_send.at[way, k], recv_sem=ring_recv.at[way, k],
            device_id={"beam": ahead if way == 0 else behind}, device_id_type=MESH)

    def weight_copy(i, j):
        return pltpu.make_async_copy(
            w_ref.at[i, :, pl.ds(j * kq, kq)], weights.at[:, pl.ds((2 * j + i) * kq, kq)], w_sem.at[i, j])

    def count_copy(r):
        return pltpu.make_async_remote_copy(
            src_ref=flags, dst_ref=counts.at[r - 1], send_sem=cnt_send.at[r - 1], recv_sem=cnt_recv.at[r - 1],
            device_id={"elem": lax.rem(me_e + r, ne)}, device_id_type=MESH)

    def chip(i):
        return lax.rem(mine + i, ways)

    def first_copy(u, i):
        rows = rows_of(u)
        return pltpu.make_async_remote_copy(
            src_ref=xpart.at[place(u), i - 1, 1 - core, rows], dst_ref=first.at[place(u), i - 1, rows],
            send_sem=first_send.at[u, i - 1], recv_sem=first_recv.at[u, i - 1],
            device_id={"elem": partner}, device_id_type=MESH)

    def second_copy(u, i):
        rows = rows_of(u)
        return pltpu.make_async_remote_copy(
            src_ref=first.at[place(u), i - 1, rows], dst_ref=second.at[place(u), i - 1, rows],
            send_sem=second_send.at[u, i - 1], recv_sem=second_recv.at[u, i - 1],
            device_id={"elem": 2 * chip(i) + core}, device_id_type=MESH)

    def own_copy(p):
        return pltpu.make_async_remote_copy(
            src_ref=opart.at[p, 1 - core], dst_ref=ofirst.at[p],
            send_sem=ofirst_send.at[p], recv_sem=ofirst_recv.at[p],
            device_id={"elem": partner}, device_id_type=MESH)

    own_in = pltpu.make_async_copy(s_ref, blocks.at[0], s_sem)
    flag_in = pltpu.make_async_copy(flag_ref, flags, f_sem)
    flag_in.start()
    own_in.start()

    barrier = pltpu.get_barrier_semaphore()
    for b in (ahead, behind):
        pl.semaphore_signal(barrier, inc=1, device_id={"beam": b}, device_id_type=MESH)
    for r in range(1, ne):
        pl.semaphore_signal(barrier, inc=1, device_id={"elem": lax.rem(me_e + r, ne)}, device_id_type=MESH)
    pl.semaphore_wait(barrier, 2 + ne - 1)

    arrived = {((0, 0), j) for j in range(q)}
    sent = [0, 0]

    def send_ready():
        for way in (0, 1):
            while sent[way] < len(arrivals[way]):
                d, j = arrivals[way][sent[way]]
                if d > 1 and ((way, d - 1), j) not in arrived:
                    break
                ring_copy(way, d, j).start()
                sent[way] += 1

    send_ready()
    for j in range(q):
        for i in (0, 1):
            weight_copy(i, j).start()

    flag_in.wait()
    for r in range(1, ne):
        count_copy(r).start()
    mask[...] = jnp.broadcast_to(flags[...].astype(jnp.float32).astype(jnp.bfloat16), mask.shape)
    own_in.wait()

    def right_of(block):
        return 0 if block == (0, half) else slot_of(*block) - (slot_of(*block) > half)

    def stage(block, j):
        slot, place = slot_of(*block), right_of(block)
        columns = pl.ds(j * kq, kq)
        re = blocks[slot, 0, :, columns] * mask[:, columns]
        im = blocks[slot, 1, :, columns] * mask[:, columns]
        left, right = pl.ds(2 * j * kq, kq), pl.ds((2 * j + 1) * kq, kq)
        rhs[place, :tb, left] = re
        rhs[place, tb:, left] = im
        rhs[place, :tb, right] = -im
        rhs[place, tb:, right] = re

    weights_here = set()

    def need(j0, j1):
        for j in range(j0, j1):
            if j not in weights_here:
                weights_here.add(j)
                for i in (0, 1):
                    weight_copy(i, j).wait()

    def apart(step):
        @pl.loop(0, 1 + me_e // ne)
        def _(_):
            step()

    def product(rows, columns, j0, j1):
        ks = pl.ds(2 * j0 * kq, 2 * (j1 - j0) * kq)
        right = jnp.concatenate([rhs[right_of(b), :, ks] for b in columns], axis=0)
        return lax.dot_general(weights[rows, ks], right, (((1,), (1,)), ((), ())),
                               preferred_element_type=jnp.float32)

    def put(ref, index, value, fresh):
        if fresh:
            ref[index] = value
        else:
            ref[index] += value

    def fold(value):
        lane = lax.broadcasted_iota(jnp.int32, (mo // 2, LANES), 1)
        return jnp.where(lane < blk, value[:mo // 2], value[mo // 2:])

    def x_store(u, i, o, value, fresh):
        put(xpart, (place(u), i - 1, o, rows_of(u)), fold(value) if folded(u) else value, fresh)

    def x_slice(d, j0, j1, fresh, final):
        need(j0, j1)
        units = units_of(d)
        columns = [b for u in units for b in unit_columns(u)]

        def part(i, o):
            rows = pl.ds(pl.multiple_of((2 * chip(i) + o) * mo, mo), mo)
            result = product(rows, columns, j0, j1)
            for n, u in enumerate(units):
                x_store(u, i, o, result[:, n * LANES:(n + 1) * LANES], fresh)

        def both(i):
            rows = pl.ds(pl.multiple_of(2 * chip(i) * mo, 2 * mo), 2 * mo)
            result = product(rows, columns, j0, j1)
            for n, u in enumerate(units):
                for o in (0, 1):
                    x_store(u, i, o, result[o * mo:(o + 1) * mo, n * LANES:(n + 1) * LANES], fresh)

        for i in range(1, ways):
            if final:
                apart(functools.partial(part, i, 1 - core))
                for u in units:
                    first_copy(u, i).start()
                apart(functools.partial(part, i, core))
            else:
                apart(functools.partial(both, i))

    def own_slice(g, j0, j1, fresh, final):
        need(j0, j1)
        pairs = [p for p in (2 * g, 2 * g + 1) if p < half]
        columns = [b for p in pairs for b in pair_columns(p)]

        def part(o):
            rows = pl.ds(pl.multiple_of((2 * mine + o) * mo, mo), mo)
            result = product(rows, columns, j0, j1)
            for n, p in enumerate(pairs):
                put(opart, (p, o), result[:, n * LANES:(n + 1) * LANES], fresh)

        def both():
            rows = pl.ds(pl.multiple_of(2 * mine * mo, 2 * mo), 2 * mo)
            result = product(rows, columns, j0, j1)
            for n, p in enumerate(pairs):
                for o in (0, 1):
                    put(opart, (p, o), result[o * mo:(o + 1) * mo, n * LANES:(n + 1) * LANES], fresh)

        if final:
            apart(functools.partial(part, 1 - core))
            for p in pairs:
                own_copy(p).start()
            apart(functools.partial(part, core))
        else:
            apart(both)

    def own_run(g, j0, j1):
        for j in range(j0, j1, step):
            own_slice(g, j, j + step, j == 0, j + step == q)

    def pass_on(d):
        for i in range(1, ways):
            for u in units_of(d):
                rows = rows_of(u)
                first_copy(u, i).wait_recv()
                first[place(u), i - 1, rows] += xpart[place(u), i - 1, core, rows]
                second_copy(u, i).start()

    def make_selection():
        row = lax.broadcasted_iota(jnp.int32, (blk, 2 * snaps), 0)
        column = lax.broadcasted_iota(jnp.int32, (blk, 2 * snaps), 1)
        offset = column - jnp.where(row < tb, row, row - tb + snaps)
        for p in range(half):
            for n, (way, d) in enumerate(pair_columns(p)):
                source = lookup(order, lax.rem(pos + (d if way else nb - d), nb))
                select[p * LANES + n * blk:p * LANES + (n + 1) * blk, :] = jnp.where(
                    offset == source * tb, 1.0, 0.0).astype(jnp.bfloat16)

    def live_gain():
        live = flags[...].astype(jnp.float32)
        for r in range(1, ne):
            count_copy(r).wait()
            live = live + counts[r - 1].astype(jnp.float32)
        return jnp.sqrt(jnp.float32(depth * ne) / jnp.sum(live, axis=1, keepdims=True))

    received = set()

    def unit_sum(u):
        for i in range(1, ways):
            if (u, i) not in received:
                received.add((u, i))
                second_copy(u, i).wait_recv()
        total = second[place(u), 0, rows_of(u)]
        for i in range(2, ways):
            total = total + second[place(u), i - 1, rows_of(u)]
        return total

    def finish(p, gain):
        own_copy(p).wait_recv()
        total = opart[p, core] + ofirst[p]
        if p == 0:
            total = total + unit_sum(0)
        else:
            left, right = unit_sum(p), unit_sum(p + 1)
            if folded(p):
                left = jnp.concatenate([left, pltpu.roll(left, blk, 1)], axis=0)
            if folded(p + 1):
                right = jnp.concatenate([pltpu.roll(right, blk, 1), right], axis=0)
            lane = lax.broadcasted_iota(jnp.int32, (mo, LANES), 1)
            total = total + jnp.where(lane < blk, left, right)
        total = total * gain
        put(square, (slice(None), slice(None)), total * total, p == 0)
        values[:, p * LANES:(p + 1) * LANES] = total.astype(jnp.bfloat16)

    gain = None
    groups = (half + 1) // 2
    make_selection()
    for k in range(len(arrivals[0])):
        for way in (0, 1):
            d, j = arrivals[way][k]
            ring_copy(way, d, j).wait_recv()
            arrived.add(((0 if d == half else way, d), j))
            send_ready()
        d, j = arrivals[1][k]
        if j == 0 and d > 1:
            pass_on(d - 1)
        if d < half:
            if d == 1:
                stage((0, 0), j)
            stage((0, d), j)
            stage((1, d), j)
            if (j + 1) % step == 0:
                x_slice(d, j + 1 - step, j + 1, j + 1 == step, j == q - 1)
            if d % 2 == 0 and j == q - 1 and d // 2 < groups:
                own_run(d // 2 - 1, 0, q // 2)
            if d % 2 == 1 and d > 1 and j == q // 2 - 1:
                own_run((d - 3) // 2, q // 2, q)
            if j == q - 1 and d >= 3:
                if gain is None:
                    gain = live_gain()
                for p in range(half - 2):
                    if min(p + 3, half - 1) == d:
                        finish(p, gain)
        else:
            m = j
            stage((0, half), m)
            stage((0, half), q - 1 - m)
            if m < q // 2 - 1:
                x_slice(half, m, m + 1, m == 0, False)
                x_slice(half, q - 1 - m, q - m, False, False)
            else:
                x_slice(half, m, m + 2, m == 0, True)

    pass_on(half)
    own_run(groups - 1, 0, q)
    if gain is None:
        gain = live_gain()
    for p in range(max(0, half - 2), half):
        finish(p, gain)
    for part in (0, 1):
        for rows in (slice(0, mo // 2), slice(mo // 2, mo)):
            out_ref[part, rows] = jnp.dot(values[rows], select[:, part * snaps:(part + 1) * snaps],
                                          preferred_element_type=jnp.float32).astype(jnp.bfloat16)
    power = jnp.sum(square[...].T, axis=0, keepdims=True) * (1.0 / snaps)
    pow_ref[...] = power

    for way in (0, 1):
        for d, j in arrivals[way]:
            ring_copy(way, d, j).wait_send()
    for u in range(half + 1):
        for i in range(1, ways):
            first_copy(u, i).wait_send()
            second_copy(u, i).wait_send()
    for p in range(half):
        own_copy(p).wait_send()


def body(order, ne, signals, weights, element_flags):
    nb = len(order)
    half = nb // 2
    _, depth, tb = signals.shape
    rows = weights.shape[1]
    mo = rows // ne
    q = PIECES
    ways = ne // 2
    if nb % 4 or ne % 2 or ways < 2 or 4 * tb != LANES:
        raise ValueError("unsupported mesh")
    items = q * (half - 1) + q // 2
    dma = pltpu.SemaphoreType.DMA
    anywhere = pl.BlockSpec(memory_space=pltpu.MemorySpace.HBM)
    vmem = pl.BlockSpec(memory_space=pltpu.VMEM)
    out, power = pl.pallas_call(
        functools.partial(kernel, order, ne),
        out_shape=(jax.ShapeDtypeStruct((2, mo, nb * tb), jnp.bfloat16),
                   jax.ShapeDtypeStruct((1, mo), jnp.float32)),
        in_specs=[anywhere, anywhere, anywhere],
        out_specs=(vmem, vmem),
        scratch_shapes=[
            pltpu.VMEM((nb, 2, tb, depth), jnp.bfloat16),
            pltpu.VMEM((1, depth), jnp.int32),
            pltpu.VMEM((tb, depth), jnp.bfloat16),
            pltpu.VMEM((rows, 2 * depth), jnp.bfloat16),
            pltpu.VMEM((nb - 1, 2 * tb, 2 * depth), jnp.bfloat16),
            pltpu.VMEM((half, ways - 1, 2, mo, LANES), jnp.float32),
            pltpu.VMEM((half, 2, mo, LANES), jnp.float32),
            pltpu.VMEM((half, ways - 1, mo, LANES), jnp.float32),
            pltpu.VMEM((half, mo, LANES), jnp.float32),
            pltpu.VMEM((half, ways - 1, mo, LANES), jnp.float32),
            pltpu.VMEM((ne - 1, 1, depth), jnp.int32),
            pltpu.VMEM((half * LANES, 2 * nb * tb), jnp.bfloat16),
            pltpu.VMEM((mo, half * LANES), jnp.bfloat16),
            pltpu.VMEM((mo, LANES), jnp.float32),
            dma((2, items)), dma((2, items)), dma((2, q)), dma, dma,
            dma((half + 1, ways - 1)), dma((half + 1, ways - 1)), dma((half,)), dma((half,)),
            dma((half + 1, ways - 1)), dma((half + 1, ways - 1)),
            dma((ne - 1,)), dma((ne - 1,)),
        ],
        compiler_params=pltpu.CompilerParams(
            collective_id=0, has_side_effects=True, vmem_limit_bytes=53 * 2**20),
        name="beamform",
    )(signals.transpose(0, 2, 1), element_flags.reshape(1, depth), weights)
    return out, power.reshape(mo)


def solution(mesh):
    return jax.shard_map(
        functools.partial(body, ring_order(mesh), mesh.shape["elem"]),
        mesh=mesh,
        in_specs=(P(None, "elem", "beam"), P(None, "beam", "elem"), P("elem")),
        out_specs=(P(None, ("beam", "elem"), None), P(("beam", "elem"))),
        check_vma=False,
    )
```

```python
import functools

import jax
import jax.numpy as jnp
from jax import lax
from jax.experimental import pallas as pl
from jax.experimental.pallas import tpu as pltpu
from jax.sharding import PartitionSpec as P

PIECES = 8
LANES = 128
MESH = pl.DeviceIdType.MESH


def ring_order(mesh):
    nb = mesh.shape["beam"]
    try:
        coords = [tuple(d.coords) for d in mesh.devices[:, 0]]
    except AttributeError:
        return list(range(nb))
    axes = [a for a in range(len(coords[0])) if len({c[a] for c in coords}) > 1]
    if len(axes) != 2:
        return list(range(nb))
    values = [sorted({c[a] for c in coords}) for a in axes]
    if len(values[0]) % 2:
        axes, values = axes[::-1], values[::-1]
    rows, cols = len(values[0]), len(values[1])
    if rows % 2 or rows * cols != nb:
        return list(range(nb))
    at = {(values[0].index(c[axes[0]]), values[1].index(c[axes[1]])): i for i, c in enumerate(coords)}
    path = [(0, 0)]
    for r in range(rows):
        inner = range(1, cols) if r % 2 == 0 else range(cols - 1, 0, -1)
        path += [(r, c) for c in inner]
    path += [(r, 0) for r in range(rows - 1, 0, -1)]
    return [at[p] for p in path]


def lookup(table, index):
    value = jnp.int32(table[0])
    for i in range(1, len(table)):
        value = jnp.where(index == i, jnp.int32(table[i]), value)
    return value


def kernel(order, ne, s_ref, flag_ref, w_ref, out_ref, pow_ref,
           blocks, flags, mask, weights, rhs, xpart, opart, first, ofirst, second, counts, select, values, square,
           ring_send, ring_recv, w_sem, s_sem, f_sem, first_send, first_recv, ofirst_send, ofirst_recv,
           second_send, second_recv, cnt_send, cnt_recv):
    nb = len(order)
    half = nb // 2
    _, tb, depth = s_ref.shape
    q = PIECES
    step = max(1, q // 4)
    kq = depth // q
    mo = opart.shape[2]
    ways = ne // 2
    snaps = nb * tb
    blk = 2 * tb

    me_b = lax.axis_index("beam")
    me_e = lax.axis_index("elem")
    inverse = [order.index(i) for i in range(nb)]
    pos = lookup(inverse, me_b)
    ahead = lookup([order[(inverse[i] + 1) % nb] for i in range(nb)], me_b)
    behind = lookup([order[(inverse[i] - 1) % nb] for i in range(nb)], me_b)
    core = lax.rem(me_e, 2)
    mine = me_e // 2
    partner = me_e + 1 - 2 * core

    def slot_of(way, d):
        return d if (way == 0 or d in (0, half)) else half + d

    def unit_columns(u):
        if u == 0:
            return [(0, 0), (0, 1)]
        if u == 1:
            return [(1, 1), (1, 1)]
        if u == half:
            return [(0, half), (0, half)]
        return [(1, u), (0, u)]

    def folded(u):
        return u in (1, half)

    def place(u):
        return 1 if u == half else u

    def rows_of(u):
        return pl.ds(mo // 2 if u == half else 0, mo // 2 if folded(u) else mo)

    def pair_columns(p):
        return [(0, 0), (0, 1)] if p == 0 else [(1, p), (0, p + 1)]

    def units_of(d):
        return [0, 1] if d == 1 else [d]

    low, high = q // 2, q // 2
    arrivals = [[(d, j) for d in range(1, half) for j in range(q)] + [(half, j) for j in last]
                for last in ([*range(high + 1, q), high], range(low))]
    number = [{item: k for k, item in enumerate(a)} for a in arrivals]

    def ring_copy(way, d, j):
        k = number[way][(d, j)]
        return pltpu.make_async_remote_copy(
            src_ref=blocks.at[0 if d == 1 else slot_of(way, d - 1)].at[:, :, pl.ds(j * kq, kq)],
            dst_ref=blocks.at[slot_of(way, d), :, :, pl.ds(j * kq, kq)],
            send_sem=ring_send.at[way, k], recv_sem=ring_recv.at[way, k],
            device_id={"beam": ahead if way == 0 else behind}, device_id_type=MESH)

    def weight_copy(i, j):
        return pltpu.make_async_copy(
            w_ref.at[i, :, pl.ds(j * kq, kq)], weights.at[:, pl.ds((2 * j + i) * kq, kq)], w_sem.at[i, j])

    def count_copy(r):
        return pltpu.make_async_remote_copy(
            src_ref=flags, dst_ref=counts.at[r - 1], send_sem=cnt_send.at[r - 1], recv_sem=cnt_recv.at[r - 1],
            device_id={"elem": lax.rem(me_e + r, ne)}, device_id_type=MESH)

    def chip(i):
        return lax.rem(mine + i, ways)

    def first_copy(u, i):
        rows = rows_of(u)
        return pltpu.make_async_remote_copy(
            src_ref=xpart.at[place(u), i - 1, 1 - core, rows], dst_ref=first.at[place(u), i - 1, rows],
            send_sem=first_send.at[u, i - 1], recv_sem=first_recv.at[u, i - 1],
            device_id={"elem": partner}, device_id_type=MESH)

    def second_copy(u, i):
        rows = rows_of(u)
        return pltpu.make_async_remote_copy(
            src_ref=first.at[place(u), i - 1, rows], dst_ref=second.at[place(u), i - 1, rows],
            send_sem=second_send.at[u, i - 1], recv_sem=second_recv.at[u, i - 1],
            device_id={"elem": 2 * chip(i) + core}, device_id_type=MESH)

    def own_copy(p):
        return pltpu.make_async_remote_copy(
            src_ref=opart.at[p, 1 - core], dst_ref=ofirst.at[p],
            send_sem=ofirst_send.at[p], recv_sem=ofirst_recv.at[p],
            device_id={"elem": partner}, device_id_type=MESH)

    own_in = pltpu.make_async_copy(s_ref, blocks.at[0], s_sem)
    flag_in = pltpu.make_async_copy(flag_ref, flags, f_sem)
    own_in.start()
    flag_in.start()
    for j in range(q):
        for i in (0, 1):
            weight_copy(i, j).start()

    barrier = pltpu.get_barrier_semaphore()
    for b in (ahead, behind):
        pl.semaphore_signal(barrier, inc=1, device_id={"beam": b}, device_id_type=MESH)
    for r in range(1, ne):
        pl.semaphore_signal(barrier, inc=1, device_id={"elem": lax.rem(me_e + r, ne)}, device_id_type=MESH)
    own_in.wait()
    pl.semaphore_wait(barrier, 2 + ne - 1)

    arrived = {((0, 0), j) for j in range(q)}
    sent = [0, 0]

    def send_ready():
        for way in (0, 1):
            while sent[way] < len(arrivals[way]):
                d, j = arrivals[way][sent[way]]
                if d > 1 and ((way, d - 1), j) not in arrived:
                    break
                ring_copy(way, d, j).start()
                sent[way] += 1

    send_ready()
    flag_in.wait()
    for r in range(1, ne):
        count_copy(r).start()
    mask[...] = jnp.broadcast_to(flags[...].astype(jnp.float32).astype(jnp.bfloat16), mask.shape)

    def right_of(block):
        return 0 if block == (0, half) else slot_of(*block) - (slot_of(*block) > half)

    def stage(block, j):
        slot, place = slot_of(*block), right_of(block)
        columns = pl.ds(j * kq, kq)
        re = blocks[slot, 0, :, columns] * mask[:, columns]
        im = blocks[slot, 1, :, columns] * mask[:, columns]
        left, right = pl.ds(2 * j * kq, kq), pl.ds((2 * j + 1) * kq, kq)
        rhs[place, :tb, left] = re
        rhs[place, tb:, left] = im
        rhs[place, :tb, right] = -im
        rhs[place, tb:, right] = re

    weights_here = set()

    def need(j0, j1):
        for j in range(j0, j1):
            if j not in weights_here:
                weights_here.add(j)
                for i in (0, 1):
                    weight_copy(i, j).wait()

    def apart(step):
        @pl.loop(0, 1 + me_e // ne)
        def _(_):
            step()

    def product(rows, columns, j0, j1):
        ks = pl.ds(2 * j0 * kq, 2 * (j1 - j0) * kq)
        right = jnp.concatenate([rhs[right_of(b), :, ks] for b in columns], axis=0)
        return lax.dot_general(weights[rows, ks], right, (((1,), (1,)), ((), ())),
                               preferred_element_type=jnp.float32)

    def put(ref, index, value, fresh):
        if fresh:
            ref[index] = value
        else:
            ref[index] += value

    def fold(value):
        lane = lax.broadcasted_iota(jnp.int32, (mo // 2, LANES), 1)
        return jnp.where(lane < blk, value[:mo // 2], value[mo // 2:])

    def x_store(u, i, o, value, fresh):
        put(xpart, (place(u), i - 1, o, rows_of(u)), fold(value) if folded(u) else value, fresh)

    def x_slice(d, j0, j1, fresh, final):
        need(j0, j1)
        units = units_of(d)
        columns = [b for u in units for b in unit_columns(u)]

        def part(i, o):
            rows = pl.ds(pl.multiple_of((2 * chip(i) + o) * mo, mo), mo)
            result = product(rows, columns, j0, j1)
            for n, u in enumerate(units):
                x_store(u, i, o, result[:, n * LANES:(n + 1) * LANES], fresh)

        def both(i):
            rows = pl.ds(pl.multiple_of(2 * chip(i) * mo, 2 * mo), 2 * mo)
            result = product(rows, columns, j0, j1)
            for n, u in enumerate(units):
                for o in (0, 1):
                    x_store(u, i, o, result[o * mo:(o + 1) * mo, n * LANES:(n + 1) * LANES], fresh)

        for i in range(1, ways):
            if final:
                apart(functools.partial(part, i, 1 - core))
                for u in units:
                    first_copy(u, i).start()
                apart(functools.partial(part, i, core))
            else:
                apart(functools.partial(both, i))

    def own_slice(g, j0, j1, fresh, final, cuts=1):
        need(j0, j1)
        size = (j1 - j0) // cuts
        pairs = [p for p in (2 * g, 2 * g + 1) if p < half]
        columns = [b for p in pairs for b in pair_columns(p)]

        def part(o, j):
            rows = pl.ds(pl.multiple_of((2 * mine + o) * mo, mo), mo)
            result = product(rows, columns, j, j + size)
            for n, p in enumerate(pairs):
                put(opart, (p, o), result[:, n * LANES:(n + 1) * LANES], fresh)

        def both():
            rows = pl.ds(pl.multiple_of(2 * mine * mo, 2 * mo), 2 * mo)
            result = product(rows, columns, j0, j1)
            for n, p in enumerate(pairs):
                for o in (0, 1):
                    put(opart, (p, o), result[o * mo:(o + 1) * mo, n * LANES:(n + 1) * LANES], fresh)

        if final:
            for j in range(j0, j1, size):
                apart(functools.partial(part, 1 - core, j))
            for p in pairs:
                own_copy(p).start()
            for j in range(j0, j1, size):
                apart(functools.partial(part, core, j))
        else:
            apart(both)

    def own_run(g, j0, j1):
        for j in range(j0, j1, step):
            own_slice(g, j, j + step, j == 0, j + step == q)

    def pass_on(d):
        for i in range(1, ways):
            for u in units_of(d):
                rows = rows_of(u)
                first_copy(u, i).wait_recv()
                first[place(u), i - 1, rows] += xpart[place(u), i - 1, core, rows]
                second_copy(u, i).start()

    def make_selection():
        row = lax.broadcasted_iota(jnp.int32, (blk, 2 * snaps), 0)
        column = lax.broadcasted_iota(jnp.int32, (blk, 2 * snaps), 1)
        offset = column - jnp.where(row < tb, row, row - tb + snaps)
        for p in range(half):
            for n, (way, d) in enumerate(pair_columns(p)):
                source = lookup(order, lax.rem(pos + (d if way else nb - d), nb))
                select[p * LANES + n * blk:p * LANES + (n + 1) * blk, :] = jnp.where(
                    offset == source * tb, 1.0, 0.0).astype(jnp.bfloat16)

    def live_gain():
        live = flags[...].astype(jnp.float32)
        for r in range(1, ne):
            count_copy(r).wait()
            live = live + counts[r - 1].astype(jnp.float32)
        return jnp.sqrt(jnp.float32(depth * ne) / jnp.sum(live, axis=1, keepdims=True))

    received = set()

    def unit_sum(u):
        for i in range(1, ways):
            if (u, i) not in received:
                received.add((u, i))
                second_copy(u, i).wait_recv()
        total = second[place(u), 0, rows_of(u)]
        for i in range(2, ways):
            total = total + second[place(u), i - 1, rows_of(u)]
        return total

    def finish(p, gain):
        own_copy(p).wait_recv()
        total = opart[p, core] + ofirst[p]
        if p == 0:
            total = total + unit_sum(0)
        else:
            left, right = unit_sum(p), unit_sum(p + 1)
            if folded(p):
                left = jnp.concatenate([left, pltpu.roll(left, blk, 1)], axis=0)
            if folded(p + 1):
                right = jnp.concatenate([pltpu.roll(right, blk, 1), right], axis=0)
            lane = lax.broadcasted_iota(jnp.int32, (mo, LANES), 1)
            total = total + jnp.where(lane < blk, left, right)
        total = total * gain
        put(square, (slice(None), slice(None)), total * total, p == 0)
        values[:, p * LANES:(p + 1) * LANES] = total.astype(jnp.bfloat16)

    def sends_done(d):
        for way in (0, 1):
            for item in arrivals[way]:
                if item[0] == d:
                    ring_copy(way, *item).wait_send()

    gain = None
    groups = (half + 1) // 2
    make_selection()
    for k in range(len(arrivals[0])):
        for way in (0, 1):
            d, j = arrivals[way][k]
            ring_copy(way, d, j).wait_recv()
            arrived.add(((0 if d == half else way, d), j))
            send_ready()
        d, j = arrivals[1][k]
        if d < half:
            if d == 1:
                stage((0, 0), j)
            stage((0, d), j)
            stage((1, d), j)
            if (j + 1) % step == 0:
                x_slice(d, j + 1 - step, j + 1, j + 1 == step, j == q - 1)
            if d % 2 == 0 and j == q - 1 and d // 2 < groups:
                own_run(d // 2 - 1, 0, q // 2)
            if d % 2 == 1 and d > 1 and j == q // 2 - 1:
                own_run((d - 3) // 2, q // 2, q)
            if j == q - 1 and d >= 3:
                if gain is None:
                    gain = live_gain()
                for p in range(half - 2):
                    if min(p + 3, half - 1) == d:
                        finish(p, gain)
            if j == q - 1:
                pass_on(d)
                sends_done(d - 1)
        else:
            m, n = j, arrivals[0][k][1]
            stage((0, half), m)
            stage((0, half), n)
            if n > high:
                x_slice(half, m, m + 1, m == 0, False)
                x_slice(half, n, n + 1, False, False)
            else:
                x_slice(half, m, m + 2, m == 0, True)

    pass_on(half)
    own_run(groups - 1, 0, q // 2)
    own_slice(groups - 1, q // 2, q, False, True, 2)
    for d in (half - 1, half):
        sends_done(d)
    for u in range(half + 1):
        for i in range(1, ways):
            first_copy(u, i).wait_send()
    if gain is None:
        gain = live_gain()
    for p in range(max(0, half - 2), half):
        finish(p, gain)
    for part in (0, 1):
        for rows in (slice(0, mo // 2), slice(mo // 2, mo)):
            out_ref[part, rows] = jnp.dot(values[rows], select[:, part * snaps:(part + 1) * snaps],
                                          preferred_element_type=jnp.float32).astype(jnp.bfloat16)
    power = jnp.sum(square[...].T, axis=0, keepdims=True) * (1.0 / snaps)
    pow_ref[...] = power

    for u in range(half + 1):
        for i in range(1, ways):
            second_copy(u, i).wait_send()
    for p in range(half):
        own_copy(p).wait_send()


def body(order, ne, signals, weights, element_flags):
    nb = len(order)
    half = nb // 2
    _, depth, tb = signals.shape
    rows = weights.shape[1]
    mo = rows // ne
    q = PIECES
    ways = ne // 2
    if nb % 4 or ne % 2 or ways < 2 or 4 * tb != LANES:
        raise ValueError("unsupported mesh")
    items = q * (half - 1) + q // 2
    dma = pltpu.SemaphoreType.DMA
    anywhere = pl.BlockSpec(memory_space=pltpu.MemorySpace.HBM)
    vmem = pl.BlockSpec(memory_space=pltpu.VMEM)
    out, power = pl.pallas_call(
        functools.partial(kernel, order, ne),
        out_shape=(jax.ShapeDtypeStruct((2, mo, nb * tb), jnp.bfloat16),
                   jax.ShapeDtypeStruct((1, mo), jnp.float32)),
        in_specs=[anywhere, anywhere, anywhere],
        out_specs=(vmem, vmem),
        scratch_shapes=[
            pltpu.VMEM((nb, 2, tb, depth), jnp.bfloat16),
            pltpu.VMEM((1, depth), jnp.int32),
            pltpu.VMEM((tb, depth), jnp.bfloat16),
            pltpu.VMEM((rows, 2 * depth), jnp.bfloat16),
            pltpu.VMEM((nb - 1, 2 * tb, 2 * depth), jnp.bfloat16),
            pltpu.VMEM((half, ways - 1, 2, mo, LANES), jnp.float32),
            pltpu.VMEM((half, 2, mo, LANES), jnp.float32),
            pltpu.VMEM((half, ways - 1, mo, LANES), jnp.float32),
            pltpu.VMEM((half, mo, LANES), jnp.float32),
            pltpu.VMEM((half, ways - 1, mo, LANES), jnp.float32),
            pltpu.VMEM((ne - 1, 1, depth), jnp.int32),
            pltpu.VMEM((half * LANES, 2 * nb * tb), jnp.bfloat16),
            pltpu.VMEM((mo, half * LANES), jnp.bfloat16),
            pltpu.VMEM((mo, LANES), jnp.float32),
            dma((2, items)), dma((2, items)), dma((2, q)), dma, dma,
            dma((half + 1, ways - 1)), dma((half + 1, ways - 1)), dma((half,)), dma((half,)),
            dma((half + 1, ways - 1)), dma((half + 1, ways - 1)),
            dma((ne - 1,)), dma((ne - 1,)),
        ],
        compiler_params=pltpu.CompilerParams(
            collective_id=0, has_side_effects=True, vmem_limit_bytes=53 * 2**20),
        name="beamform",
    )(signals.transpose(0, 2, 1), element_flags.reshape(1, depth), weights)
    return out, power.reshape(mo)


def solution(mesh):
    return jax.shard_map(
        functools.partial(body, ring_order(mesh), mesh.shape["elem"]),
        mesh=mesh,
        in_specs=(P(None, "elem", "beam"), P(None, "beam", "elem"), P("elem")),
        out_specs=(P(None, ("beam", "elem"), None), P(("beam", "elem"))),
        check_vma=False,
    )
```

```python
import functools

import jax
import jax.numpy as jnp
from jax import lax
from jax.experimental import pallas as pl
from jax.experimental.pallas import tpu as pltpu
from jax.sharding import PartitionSpec as P

PIECES = 8
LANES = 128
MESH = pl.DeviceIdType.MESH


def ring_order(mesh):
    nb = mesh.shape["beam"]
    try:
        coords = [tuple(d.coords) for d in mesh.devices[:, 0]]
    except AttributeError:
        return list(range(nb))
    axes = [a for a in range(len(coords[0])) if len({c[a] for c in coords}) > 1]
    if len(axes) != 2:
        return list(range(nb))
    values = [sorted({c[a] for c in coords}) for a in axes]
    if len(values[0]) % 2:
        axes, values = axes[::-1], values[::-1]
    rows, cols = len(values[0]), len(values[1])
    if rows % 2 or rows * cols != nb:
        return list(range(nb))
    at = {(values[0].index(c[axes[0]]), values[1].index(c[axes[1]])): i for i, c in enumerate(coords)}
    path = [(0, 0)]
    for r in range(rows):
        inner = range(1, cols) if r % 2 == 0 else range(cols - 1, 0, -1)
        path += [(r, c) for c in inner]
    path += [(r, 0) for r in range(rows - 1, 0, -1)]
    return [at[p] for p in path]


def lookup(table, index):
    value = jnp.int32(table[0])
    for i in range(1, len(table)):
        value = jnp.where(index == i, jnp.int32(table[i]), value)
    return value


def kernel(order, ne, s_ref, flag_ref, w_ref, out_ref, pow_ref,
           blocks, flags, mask, weights, rhs, xpart, opart, first, ofirst, second, counts, select, values, square,
           ring_send, ring_recv, w_sem, s_sem, f_sem, first_send, first_recv, ofirst_send, ofirst_recv,
           second_send, second_recv, cnt_send, cnt_recv):
    nb = len(order)
    half = nb // 2
    _, tb, depth = s_ref.shape
    q = PIECES
    step = max(1, q // 4)
    kq = depth // q
    mo = opart.shape[2]
    ways = ne // 2
    snaps = nb * tb
    blk = 2 * tb

    me_b = lax.axis_index("beam")
    me_e = lax.axis_index("elem")
    inverse = [order.index(i) for i in range(nb)]
    pos = lookup(inverse, me_b)
    ahead = lookup([order[(inverse[i] + 1) % nb] for i in range(nb)], me_b)
    behind = lookup([order[(inverse[i] - 1) % nb] for i in range(nb)], me_b)
    core = lax.rem(me_e, 2)
    mine = me_e // 2
    partner = me_e + 1 - 2 * core

    def slot_of(way, d):
        return d if (way == 0 or d in (0, half)) else half + d

    def unit_columns(u):
        if u == 0:
            return [(0, 0), (0, 1)]
        if u == 1:
            return [(1, 1), (1, 1)]
        if u == half:
            return [(0, half), (0, half)]
        return [(1, u), (0, u)]

    def folded(u):
        return u in (1, half)

    def place(u):
        return 1 if u == half else u

    def rows_of(u):
        return pl.ds(mo // 2 if u == half else 0, mo // 2 if folded(u) else mo)

    def pair_columns(p):
        return [(0, 0), (0, 1)] if p == 0 else [(1, p), (0, p + 1)]

    def units_of(d):
        return [0, 1] if d == 1 else [d]

    low, high = q // 2, q // 2
    arrivals = [[(d, j) for d in range(1, half) for j in range(q)] + [(half, j) for j in last]
                for last in ([*range(high + 1, q), high], range(low))]
    number = [{item: k for k, item in enumerate(a)} for a in arrivals]

    def ring_copy(way, d, j):
        k = number[way][(d, j)]
        return pltpu.make_async_remote_copy(
            src_ref=blocks.at[0 if d == 1 else slot_of(way, d - 1)].at[:, :, pl.ds(j * kq, kq)],
            dst_ref=blocks.at[slot_of(way, d), :, :, pl.ds(j * kq, kq)],
            send_sem=ring_send.at[way, k], recv_sem=ring_recv.at[way, k],
            device_id={"beam": ahead if way == 0 else behind}, device_id_type=MESH)

    def weight_copy(i, j):
        return pltpu.make_async_copy(
            w_ref.at[i, :, pl.ds(j * kq, kq)], weights.at[:, pl.ds((2 * j + i) * kq, kq)], w_sem.at[i, j])

    def count_copy(r):
        return pltpu.make_async_remote_copy(
            src_ref=flags, dst_ref=counts.at[r - 1], send_sem=cnt_send.at[r - 1], recv_sem=cnt_recv.at[r - 1],
            device_id={"elem": lax.rem(me_e + r, ne)}, device_id_type=MESH)

    def chip(i):
        return lax.rem(mine + i, ways)

    def first_copy(u, i):
        rows = rows_of(u)
        return pltpu.make_async_remote_copy(
            src_ref=xpart.at[place(u), i - 1, 1 - core, rows], dst_ref=first.at[place(u), i - 1, rows],
            send_sem=first_send.at[u, i - 1], recv_sem=first_recv.at[u, i - 1],
            device_id={"elem": partner}, device_id_type=MESH)

    def second_copy(u, i):
        rows = rows_of(u)
        return pltpu.make_async_remote_copy(
            src_ref=first.at[place(u), i - 1, rows], dst_ref=second.at[place(u), i - 1, rows],
            send_sem=second_send.at[u, i - 1], recv_sem=second_recv.at[u, i - 1],
            device_id={"elem": 2 * chip(i) + core}, device_id_type=MESH)

    def own_copy(p):
        return pltpu.make_async_remote_copy(
            src_ref=opart.at[p, 1 - core], dst_ref=ofirst.at[p],
            send_sem=ofirst_send.at[p], recv_sem=ofirst_recv.at[p],
            device_id={"elem": partner}, device_id_type=MESH)

    own_in = pltpu.make_async_copy(s_ref, blocks.at[0], s_sem)
    flag_in = pltpu.make_async_copy(flag_ref, flags, f_sem)
    flag_in.start()
    own_in.start()

    barrier = pltpu.get_barrier_semaphore()
    for b in (ahead, behind):
        pl.semaphore_signal(barrier, inc=1, device_id={"beam": b}, device_id_type=MESH)
    for r in range(1, ne):
        pl.semaphore_signal(barrier, inc=1, device_id={"elem": lax.rem(me_e + r, ne)}, device_id_type=MESH)
    flag_in.wait()
    own_in.wait()
    for j in range(q):
        for i in (0, 1):
            weight_copy(i, j).start()
    pl.semaphore_wait(barrier, 2 + ne - 1)

    arrived = {((0, 0), j) for j in range(q)}
    sent = [0, 0]

    def send_ready():
        for way in (0, 1):
            while sent[way] < len(arrivals[way]):
                d, j = arrivals[way][sent[way]]
                if d > 1 and ((way, d - 1), j) not in arrived:
                    break
                ring_copy(way, d, j).start()
                sent[way] += 1

    send_ready()
    for r in range(1, ne):
        count_copy(r).start()
    mask[...] = jnp.broadcast_to(flags[...].astype(jnp.float32).astype(jnp.bfloat16), mask.shape)

    def right_of(block):
        return 0 if block == (0, half) else slot_of(*block) - (slot_of(*block) > half)

    def stage(block, j):
        slot, place = slot_of(*block), right_of(block)
        columns = pl.ds(j * kq, kq)
        re = blocks[slot, 0, :, columns] * mask[:, columns]
        im = blocks[slot, 1, :, columns] * mask[:, columns]
        left, right = pl.ds(2 * j * kq, kq), pl.ds((2 * j + 1) * kq, kq)
        rhs[place, :tb, left] = re
        rhs[place, tb:, left] = im
        rhs[place, :tb, right] = -im
        rhs[place, tb:, right] = re

    weights_here = set()

    def need(j0, j1):
        for j in range(j0, j1):
            if j not in weights_here:
                weights_here.add(j)
                for i in (0, 1):
                    weight_copy(i, j).wait()

    def apart(step):
        @pl.loop(0, 1 + me_e // ne)
        def _(_):
            step()

    def product(rows, columns, j0, j1):
        ks = pl.ds(2 * j0 * kq, 2 * (j1 - j0) * kq)
        right = jnp.concatenate([rhs[right_of(b), :, ks] for b in columns], axis=0)
        return lax.dot_general(weights[rows, ks], right, (((1,), (1,)), ((), ())),
                               preferred_element_type=jnp.float32)

    def put(ref, index, value, fresh):
        if fresh:
            ref[index] = value
        else:
            ref[index] += value

    def fold(value):
        lane = lax.broadcasted_iota(jnp.int32, (mo // 2, LANES), 1)
        return jnp.where(lane < blk, value[:mo // 2], value[mo // 2:])

    def x_store(u, i, o, value, fresh):
        put(xpart, (place(u), i - 1, o, rows_of(u)), fold(value) if folded(u) else value, fresh)

    def x_slice(d, j0, j1, fresh, final):
        need(j0, j1)
        units = units_of(d)
        columns = [b for u in units for b in unit_columns(u)]

        def part(i, o):
            rows = pl.ds(pl.multiple_of((2 * chip(i) + o) * mo, mo), mo)
            result = product(rows, columns, j0, j1)
            for n, u in enumerate(units):
                x_store(u, i, o, result[:, n * LANES:(n + 1) * LANES], fresh)

        def both(i):
            rows = pl.ds(pl.multiple_of(2 * chip(i) * mo, 2 * mo), 2 * mo)
            result = product(rows, columns, j0, j1)
            for n, u in enumerate(units):
                for o in (0, 1):
                    x_store(u, i, o, result[o * mo:(o + 1) * mo, n * LANES:(n + 1) * LANES], fresh)

        for i in range(1, ways):
            if final:
                apart(functools.partial(part, i, 1 - core))
                for u in units:
                    first_copy(u, i).start()
                apart(functools.partial(part, i, core))
            else:
                apart(functools.partial(both, i))

    def own_slice(g, j0, j1, fresh, final, cuts=1):
        need(j0, j1)
        size = (j1 - j0) // cuts
        pairs = [p for p in (2 * g, 2 * g + 1) if p < half]
        columns = [b for p in pairs for b in pair_columns(p)]

        def part(o, j):
            rows = pl.ds(pl.multiple_of((2 * mine + o) * mo, mo), mo)
            result = product(rows, columns, j, j + size)
            for n, p in enumerate(pairs):
                put(opart, (p, o), result[:, n * LANES:(n + 1) * LANES], fresh)

        def both():
            rows = pl.ds(pl.multiple_of(2 * mine * mo, 2 * mo), 2 * mo)
            result = product(rows, columns, j0, j1)
            for n, p in enumerate(pairs):
                for o in (0, 1):
                    put(opart, (p, o), result[o * mo:(o + 1) * mo, n * LANES:(n + 1) * LANES], fresh)

        if final:
            for j in range(j0, j1, size):
                apart(functools.partial(part, 1 - core, j))
            for p in pairs:
                own_copy(p).start()
            for j in range(j0, j1, size):
                apart(functools.partial(part, core, j))
        else:
            apart(both)

    def own_run(g, j0, j1):
        for j in range(j0, j1, step):
            own_slice(g, j, j + step, j == 0, j + step == q)

    def pass_on(d):
        for i in range(1, ways):
            for u in units_of(d):
                rows = rows_of(u)
                first_copy(u, i).wait_recv()
                first[place(u), i - 1, rows] += xpart[place(u), i - 1, core, rows]
                second_copy(u, i).start()

    def make_selection():
        row = lax.broadcasted_iota(jnp.int32, (blk, 2 * snaps), 0)
        column = lax.broadcasted_iota(jnp.int32, (blk, 2 * snaps), 1)
        offset = column - jnp.where(row < tb, row, row - tb + snaps)
        for p in range(half):
            for n, (way, d) in enumerate(pair_columns(p)):
                source = lookup(order, lax.rem(pos + (d if way else nb - d), nb))
                select[p * LANES + n * blk:p * LANES + (n + 1) * blk, :] = jnp.where(
                    offset == source * tb, 1.0, 0.0).astype(jnp.bfloat16)

    def live_gain():
        live = flags[...].astype(jnp.float32)
        for r in range(1, ne):
            count_copy(r).wait()
            live = live + counts[r - 1].astype(jnp.float32)
        return jnp.sqrt(jnp.float32(depth * ne) / jnp.sum(live, axis=1, keepdims=True))

    received = set()

    def unit_sum(u):
        for i in range(1, ways):
            if (u, i) not in received:
                received.add((u, i))
                second_copy(u, i).wait_recv()
        total = second[place(u), 0, rows_of(u)]
        for i in range(2, ways):
            total = total + second[place(u), i - 1, rows_of(u)]
        return total

    def finish(p, gain):
        own_copy(p).wait_recv()
        total = opart[p, core] + ofirst[p]
        if p == 0:
            total = total + unit_sum(0)
        else:
            left, right = unit_sum(p), unit_sum(p + 1)
            if folded(p):
                left = jnp.concatenate([left, pltpu.roll(left, blk, 1)], axis=0)
            if folded(p + 1):
                right = jnp.concatenate([pltpu.roll(right, blk, 1), right], axis=0)
            lane = lax.broadcasted_iota(jnp.int32, (mo, LANES), 1)
            total = total + jnp.where(lane < blk, left, right)
        total = total * gain
        put(square, (slice(None), slice(None)), total * total, p == 0)
        values[:, p * LANES:(p + 1) * LANES] = total.astype(jnp.bfloat16)

    def sends_done(d):
        for way in (0, 1):
            for item in arrivals[way]:
                if item[0] == d:
                    ring_copy(way, *item).wait_send()

    gain = None
    groups = (half + 1) // 2
    make_selection()
    for k in range(len(arrivals[0])):
        for way in (0, 1):
            d, j = arrivals[way][k]
            ring_copy(way, d, j).wait_recv()
            arrived.add(((0 if d == half else way, d), j))
            send_ready()
        d, j = arrivals[1][k]
        if d < half:
            if d == 1:
                stage((0, 0), j)
            stage((0, d), j)
            stage((1, d), j)
            if (j + 1) % step == 0:
                x_slice(d, j + 1 - step, j + 1, j + 1 == step, j == q - 1)
            if d % 2 == 0 and j == q - 1 and d // 2 < groups:
                own_run(d // 2 - 1, 0, q // 2)
            if d % 2 == 1 and d > 1 and j == q // 2 - 1:
                own_run((d - 3) // 2, q // 2, q)
            if j == q - 1 and d >= 3:
                if gain is None:
                    gain = live_gain()
                for p in range(half - 2):
                    if min(p + 3, half - 1) == d:
                        finish(p, gain)
            if j == q - 1:
                pass_on(d)
                sends_done(d - 1)
        else:
            m, n = j, arrivals[0][k][1]
            stage((0, half), m)
            stage((0, half), n)
            if n > high:
                x_slice(half, m, m + 1, m == 0, False)
                x_slice(half, n, n + 1, False, False)
            else:
                x_slice(half, m, m + 2, m == 0, True)

    pass_on(half)
    own_run(groups - 1, 0, q // 2)
    own_slice(groups - 1, q // 2, q, False, True, 2)
    for d in (half - 1, half):
        sends_done(d)
    for u in range(half + 1):
        for i in range(1, ways):
            first_copy(u, i).wait_send()
    if gain is None:
        gain = live_gain()
    for p in range(max(0, half - 2), half):
        finish(p, gain)
    for part in (0, 1):
        for rows in (slice(0, mo // 2), slice(mo // 2, mo)):
            out_ref[part, rows] = jnp.dot(values[rows], select[:, part * snaps:(part + 1) * snaps],
                                          preferred_element_type=jnp.float32).astype(jnp.bfloat16)
    power = jnp.sum(square[...].T, axis=0, keepdims=True) * (1.0 / snaps)
    pow_ref[...] = power

    for u in range(half + 1):
        for i in range(1, ways):
            second_copy(u, i).wait_send()
    for p in range(half):
        own_copy(p).wait_send()


def body(order, ne, signals, weights, element_flags):
    nb = len(order)
    half = nb // 2
    _, depth, tb = signals.shape
    rows = weights.shape[1]
    mo = rows // ne
    q = PIECES
    ways = ne // 2
    if nb % 4 or ne % 2 or ways < 2 or 4 * tb != LANES:
        raise ValueError("unsupported mesh")
    items = q * (half - 1) + q // 2
    dma = pltpu.SemaphoreType.DMA
    anywhere = pl.BlockSpec(memory_space=pltpu.MemorySpace.HBM)
    vmem = pl.BlockSpec(memory_space=pltpu.VMEM)
    out, power = pl.pallas_call(
        functools.partial(kernel, order, ne),
        out_shape=(jax.ShapeDtypeStruct((2, mo, nb * tb), jnp.bfloat16),
                   jax.ShapeDtypeStruct((1, mo), jnp.float32)),
        in_specs=[anywhere, anywhere, anywhere],
        out_specs=(vmem, vmem),
        scratch_shapes=[
            pltpu.VMEM((nb, 2, tb, depth), jnp.bfloat16),
            pltpu.VMEM((1, depth), jnp.int32),
            pltpu.VMEM((tb, depth), jnp.bfloat16),
            pltpu.VMEM((rows, 2 * depth), jnp.bfloat16),
            pltpu.VMEM((nb - 1, 2 * tb, 2 * depth), jnp.bfloat16),
            pltpu.VMEM((half, ways - 1, 2, mo, LANES), jnp.float32),
            pltpu.VMEM((half, 2, mo, LANES), jnp.float32),
            pltpu.VMEM((half, ways - 1, mo, LANES), jnp.float32),
            pltpu.VMEM((half, mo, LANES), jnp.float32),
            pltpu.VMEM((half, ways - 1, mo, LANES), jnp.float32),
            pltpu.VMEM((ne - 1, 1, depth), jnp.int32),
            pltpu.VMEM((half * LANES, 2 * nb * tb), jnp.bfloat16),
            pltpu.VMEM((mo, half * LANES), jnp.bfloat16),
            pltpu.VMEM((mo, LANES), jnp.float32),
            dma((2, items)), dma((2, items)), dma((2, q)), dma, dma,
            dma((half + 1, ways - 1)), dma((half + 1, ways - 1)), dma((half,)), dma((half,)),
            dma((half + 1, ways - 1)), dma((half + 1, ways - 1)),
            dma((ne - 1,)), dma((ne - 1,)),
        ],
        compiler_params=pltpu.CompilerParams(
            collective_id=0, has_side_effects=True, vmem_limit_bytes=53 * 2**20),
        name="beamform",
    )(signals.transpose(0, 2, 1),
      pltpu.with_memory_space_constraint(element_flags.reshape(1, depth), pltpu.MemorySpace.HBM), weights)
    return out, power.reshape(mo)


def solution(mesh):
    return jax.shard_map(
        functools.partial(body, ring_order(mesh), mesh.shape["elem"]),
        mesh=mesh,
        in_specs=(P(None, "elem", "beam"), P(None, "beam", "elem"), P("elem")),
        out_specs=(P(None, ("beam", "elem"), None), P(("beam", "elem"))),
        check_vma=False,
    )
```
